32 devices in a mesh: ckpt: 2 (over y), key: 4 (over x, core), qry: 4 (over z).
Axes of the slice: x: 2, y: 2, z: 4, core: 2. Of those that a mesh axis runs over, the one named last changes fastest.
Arguments:
- queries: bfloat16 [1024, 4096], P(('ckpt', 'qry'), 'key'), parts along dimension 0, may hold values from -8 to 8
- keys: bfloat16 [8192, 1024], P(('ckpt', 'key')), parts along dimension 0, may hold values from -8 to 8
- values: bfloat16 [8192, 1024], P(('ckpt', 'key')), parts along dimension 0, may hold values from -6 to 6
- out_grad: bfloat16 [1024, 4096], P(('ckpt', 'qry'), 'key'), parts along dimension 0, may hold values from -6 to 6
Outputs:
- attn_out: bfloat16 [1024, 4096], P(('ckpt', 'qry'), 'key'), parts along dimension 0
- query_out: bfloat16 [1024, 4096], P(('ckpt', 'qry'), 'key'), parts along dimension 0
- key_out: bfloat16 [8192, 1024], P(('ckpt', 'key'), 'qry'), parts along dimension 0
- value_out: bfloat16 [8192, 1024], P(('ckpt', 'key'), 'qry'), parts along dimension 0
The draws below stay inside these ranges and needn't reach their ends.
There are 2 independent parts, one for each index of `ckpt`. The reference program is written for one: setup_inputs(seed, part) draws one part's arguments, and reference() takes and returns one part's arrays. A program takes and returns all parts, laid end to end along the dimension named above; each array names one. Nothing has to cross between parts.
All inputs are finite; a program needn't handle non-finite values.
Results may differ from the reference program's by a relative error of at most 0.03.
Values may be sent and summed in bfloat16 or wider, within the bound.
A program may use at most 64 MiB of HBM per device.

```python
import math
import jax
import jax.numpy as jnp
from jax import lax

HQ = 32
KVH = 8
HD = 128
Q_DEV = 128
KEY_DEV = 1024
QROWS = 512
KROWS = 4096


def draw_queries(key, part):
    sample = jax.random.normal(jax.random.fold_in(key, 11), (QROWS, HQ * HD), jnp.float32)
    sample = jnp.clip(sample, -8.0, 8.0)
    return sample.astype(jnp.bfloat16)


def draw_keys(key, part):
    sample = jax.random.normal(jax.random.fold_in(key, 21), (KROWS, KVH * HD), jnp.float32)
    sample = jnp.clip(sample, -8.0, 8.0)
    return sample.astype(jnp.bfloat16)


def block_scale(own_key, shape, cuts, least, top_value):
    def one(position, shards_of):
        heights = jax.random.uniform(jax.random.fold_in(jax.random.fold_in(own_key, 6), position), (shards_of,), jnp.float32, least / len(cuts), top_value / len(cuts))
        return jnp.repeat(jnp.exp(heights), shape[position] // shards_of).reshape((-1,) + (1,) * (len(shape) - position - 1))

    level = one(*cuts[0])
    for cut in cuts[1:]:
        level = level * one(*cut)
    return level


def gaussian(own_key, extent, deviation, reach, cuts=(), dtype=jnp.bfloat16):
    result = jax.random.normal(own_key, extent, jnp.float32) * deviation
    if len(cuts) > 0:
        result = block_scale(own_key, extent, cuts, -0.22, 0.18) * result
    return jnp.clip(result, min=-reach, max=reach).astype(dtype)


def setup_inputs(seed: int = 0, part: int = 0) -> dict:
    seeds = jax.random.split(jax.random.key(seed), 5)
    own_keys = jax.random.split(jax.random.fold_in(seeds[4], part), 5)
    return {
        "queries": draw_queries(jax.random.fold_in(jax.random.fold_in(seeds[4], part), 71), part),
        "keys": draw_keys(jax.random.fold_in(jax.random.fold_in(seeds[4], part), 71), part),
        "values": gaussian(own_keys[2], (KROWS, KVH * HD), 1.0, 6.0, ((0, 4),)),
        "out_grad": gaussian(own_keys[3], (QROWS, HQ * HD), 1.0, 6.0, ((0, 4), (1, 4))),
    }


PRECISION_HIGH = lax.Precision.HIGHEST

def rounded_values(value):
    return lax.optimization_barrier(value.astype(jnp.bfloat16)).astype(jnp.float32)

def reference(queries, keys, values, out_grad):
    per_group = HQ // KVH
    factor = 1.0 / math.sqrt(HD)
    query_count = queries.shape[0]
    key_count = keys.shape[0]
    block_count = query_count // Q_DEV
    key_blocks = key_count // KEY_DEV
    query_heads = queries.reshape(block_count, Q_DEV, KVH, per_group, HD).transpose(2, 0, 3, 1, 4)
    grad_heads = out_grad.reshape(block_count, Q_DEV, KVH, per_group, HD).transpose(2, 0, 3, 1, 4)
    key_heads = keys.reshape(key_count, KVH, HD).transpose(1, 0, 2)
    value_heads = values.reshape(key_count, KVH, HD).transpose(1, 0, 2)

    def per_head(inputs):
        query_group, grad_group, key_part, value_portion = inputs
        key_float = key_part.astype(jnp.float32)
        value_float = value_portion.astype(jnp.float32)
        value_division = value_float.reshape(key_blocks, KEY_DEV, HD)

        def per_block(running, pieces):
            query_float = pieces[0].astype(jnp.float32)
            grad_float = pieces[1].astype(jnp.float32)
            logits = jnp.einsum('grd,kd->grk', query_float, key_float, precision=PRECISION_HIGH) * factor
            split = logits.reshape(logits.shape[0], logits.shape[1], key_blocks, KEY_DEV)
            block_peak = lax.optimization_barrier(jnp.max(split, axis=-1))
            exponent_terms = jnp.exp(split - block_peak[..., None])
            block_total = lax.optimization_barrier(jnp.sum(exponent_terms, axis=-1))
            block_partial_sum = jnp.einsum('wpme,mey->wpmy', rounded_values(exponent_terms), value_division, precision=PRECISION_HIGH)
            peak = lax.optimization_barrier(jnp.max(block_peak, axis=-1))
            weight = jnp.exp(block_peak - peak[..., None])
            totals = lax.optimization_barrier(jnp.sum(weight * block_total, axis=-1))
            summed = lax.optimization_barrier(jnp.sum(block_partial_sum * weight[..., None], axis=2))
            attn_block = (summed / totals[..., None]).astype(jnp.bfloat16)
            row_delta = lax.optimization_barrier(jnp.sum(grad_float * attn_block.astype(jnp.float32), axis=-1))
            log_norm = peak + jnp.log(totals)
            probs = jnp.exp(logits - log_norm[..., None])
            grad_prob = jnp.einsum('grd,kd->grk', grad_float, value_float, precision=PRECISION_HIGH)
            grad_logit = rounded_values(probs * (grad_prob - row_delta[..., None]))
            query_grad = jnp.einsum('grk,kd->grd', grad_logit, key_float, precision=PRECISION_HIGH) * factor
            key_grad = jnp.einsum('grk,grd->kd', grad_logit, query_float, precision=PRECISION_HIGH) * factor
            value_grad = jnp.einsum('grk,grd->kd', rounded_values(probs), grad_float, precision=PRECISION_HIGH)
            updated = (running[0] + rounded_values(key_grad), running[1] + rounded_values(value_grad))
            return (updated, (attn_block, query_grad.astype(jnp.bfloat16)))
        empty = jnp.zeros((key_count, HD), jnp.float32)
        sums, outputs = lax.scan(per_block, (empty, empty), (query_group, grad_group))
        return (outputs[0], outputs[1], sums[0].astype(jnp.bfloat16), sums[1].astype(jnp.bfloat16))
    attn_heads, query_grads, key_grads, value_grads = lax.map(per_head, (query_heads, grad_heads, key_heads, value_heads))
    attn_out = attn_heads.transpose(1, 3, 0, 2, 4).reshape(query_count, HQ * HD)
    query_out = query_grads.transpose(1, 3, 0, 2, 4).reshape(query_count, HQ * HD)
    key_out = key_grads.transpose(1, 0, 2).reshape(key_count, KVH * HD)
    value_out = value_grads.transpose(1, 0, 2).reshape(key_count, KVH * HD)
    return (attn_out, query_out, key_out, value_out)
```

```python
import functools
import math

import jax
import jax.numpy as jnp
from jax import lax
from jax.experimental import pallas as pl
from jax.experimental.pallas import tpu as pltpu
from jax.sharding import PartitionSpec as P

HQ = 32
KVH = 8
HD = 128
MESH = pl.DeviceIdType.MESH
F32 = jnp.float32
BF16 = jnp.bfloat16


def nt(a, b):
    return lax.dot_general(a, b, (((1,), (1,)), ((), ())), preferred_element_type=F32)


def nn(a, b):
    return lax.dot_general(a, b, (((1,), (0,)), ((), ())), preferred_element_type=F32)


def kernel(
    n_key, n_qry,
    q_ref, d_ref, k_hbm, v_hbm,
    attn_ref, dq_ref, dk_ref, dv_ref,
    qg, dg, ks, vs, kt, vt, exps, part, stat, part_in, stat_in, norm, norm_in,
    dqp, dqp_in, dk_acc, dv_acc,
    kv_sem, q_s, q_r, d_s, d_r, o_s, o_r, st_s, st_r, n_s, n_r, dq_s, dq_r,
):
    factor = 1.0 / math.sqrt(HD)
    log2e_factor = factor * math.log2(math.e)
    per_group = HQ // KVH
    r = n_key // n_qry
    nb = n_key
    rows, cols = q_ref.shape
    heads = cols // HD
    chunk = min(per_group, heads)
    ng = heads // chunk
    kv_cols = ks.shape[1]
    me_c = lax.axis_index("ckpt")
    me_k = lax.axis_index("key")
    me_q = lax.axis_index("qry")
    plane = me_k // r
    my_block = me_q * r + me_k % r
    my_step = (me_q - plane + n_qry) % n_qry

    kv_off = pl.ds(pl.multiple_of(me_q * kv_cols, HD), kv_cols)
    k_copy = pltpu.make_async_copy(k_hbm.at[:, kv_off], ks, kv_sem.at[0])
    v_copy = pltpu.make_async_copy(v_hbm.at[:, kv_off], vs, kv_sem.at[1])
    k_copy.start()
    v_copy.start()

    def is_me(k, q):
        return jnp.logical_and(me_k == k, me_q == q)

    def other(k, q):
        return jnp.logical_or(me_k != k, me_q != q)

    targets = [(k, plane) for k in range(n_key)]
    sources = [(me_q * r + j, q) for q in range(n_qry) for j in range(r)]
    barrier = pltpu.get_barrier_semaphore()
    for k, q in targets + sources:
        @pl.when(other(k, q))
        def _():
            pl.semaphore_signal(barrier, inc=1, device_id=(me_c, k, q), device_id_type=MESH)

    @pl.when(plane == me_q)
    def _():
        pl.semaphore_wait(barrier, 2 * n_key - 2)

    @pl.when(plane != me_q)
    def _():
        pl.semaphore_wait(barrier, 2 * n_key)

    def send(src, dst, ssem, rsem, k, q):
        @pl.when(is_me(k, q))
        def _():
            pltpu.make_async_copy(src, dst, rsem).start()

        @pl.when(other(k, q))
        def _():
            pltpu.make_async_remote_copy(
                src, dst, ssem, rsem, device_id=(me_c, k, q), device_id_type=MESH
            ).start()

    def sent(src, dst, ssem, rsem, k, q):
        @pl.when(other(k, q))
        def _():
            pltpu.make_async_remote_copy(
                src, dst, ssem, rsem, device_id=(me_c, k, q), device_id_type=MESH
            ).wait_send()

    def arrived(dst, rsem):
        pltpu.make_async_copy(dst, dst, rsem).wait()

    q_args = [
        (q_ref, qg.at[my_block], q_s.at[i], q_r.at[my_block], k, q)
        for i, (k, q) in enumerate(targets)
    ]
    d_args = [
        (d_ref, dg.at[my_block], d_s.at[i], d_r.at[my_block], k, q)
        for i, (k, q) in enumerate(targets)
    ]
    for args in q_args:
        send(*args)
    for args in d_args:
        send(*args)

    dk_acc[...] = jnp.zeros_like(dk_acc)
    dv_acc[...] = jnp.zeros_like(dv_acc)
    k_copy.wait()
    v_copy.wait()
    for g in range(kv_cols // HD):
        at = slice(g * HD, (g + 1) * HD)
        kt[at, :] = ks[:, at].astype(F32).T.astype(BF16)
        vt[at, :] = vs[:, at].astype(F32).T.astype(BF16)

    def stacked(ref, b, gi):
        return jnp.concatenate(
            [ref[b, :, (gi * chunk + c) * HD : (gi * chunk + c + 1) * HD] for c in range(chunk)],
            axis=0,
        )

    def o_args(b, j, qq):
        k, q = me_q * r + j, qq
        return (
            (part.at[b], part_in.at[me_k], o_s.at[b], o_r.at[me_k], k, q),
            (stat.at[b], stat_in.at[me_k], st_s.at[b], st_r.at[me_k], k, q),
            (dqp.at[b], dqp_in.at[me_k], dq_s.at[b], dq_r.at[me_k], k, q),
        )

    n_args = [
        (norm, norm_in.at[my_block], n_s.at[i], n_r.at[my_block], k, q)
        for i, (k, q) in enumerate(targets)
    ]

    def forward(b, j):
        arrived(qg.at[b], q_r.at[b])
        for gi in range(ng):
            kv = (j * heads + gi * chunk) // per_group
            at = slice(kv * HD, (kv + 1) * HD)
            scores = nt(ks[:, at], stacked(qg, b, gi))
            top = jnp.max(scores, axis=0, keepdims=True)
            terms = jnp.exp2(scores * log2e_factor - top * log2e_factor)
            total = jnp.sum(terms, axis=0, keepdims=True)
            small = terms.astype(BF16)
            exps[b, gi] = small
            out = nn(vt[at, :], small)
            for c in range(chunk):
                h = gi * chunk + c
                lanes = slice(c * rows, (c + 1) * rows)
                part[b, h * HD : (h + 1) * HD, :] = out[:, lanes].astype(BF16)
                stat[b, h : h + 1, :] = top[:, lanes] * factor
                stat[b, heads + h : heads + h + 1, :] = total[:, lanes]

    def combine():
        for k in range(n_key):
            arrived(part_in.at[k], o_r.at[k])
            arrived(stat_in.at[k], st_r.at[k])
        for h in range(heads):
            at = slice(h * HD, (h + 1) * HD)
            peaks = [stat_in[k, h : h + 1, :] for k in range(n_key)]
            peak = functools.reduce(jnp.maximum, peaks)
            weights = [jnp.exp(p - peak) for p in peaks]
            total = sum(w * stat_in[k, heads + h : heads + h + 1, :] for k, w in enumerate(weights))
            out = sum(w * part_in[k, at, :].astype(F32) for k, w in enumerate(weights)) / total
            attn = out.T.astype(BF16)
            attn_ref[:, at] = attn
            product = d_ref[:, at].astype(F32) * attn.astype(F32)
            norm[h : h + 1, :] = peak + jnp.log(total)
            norm[heads + h : heads + h + 1, :] = jnp.sum(product.T, axis=0, keepdims=True)
        for args in n_args:
            send(*args)

    def backward(b, j):
        arrived(norm_in.at[b], n_r.at[b])
        arrived(dg.at[b], d_r.at[b])
        for gi in range(ng):
            kv = (j * heads + gi * chunk) // per_group
            at = slice(kv * HD, (kv + 1) * HD)
            queries = stacked(qg, b, gi)
            grads = stacked(dg, b, gi)
            hs = [gi * chunk + c for c in range(chunk)]
            scale = jnp.concatenate(
                [jnp.exp(stat[b, h : h + 1, :] - norm_in[b, h : h + 1, :]) for h in hs], axis=1
            )
            delta = jnp.concatenate(
                [norm_in[b, heads + h : heads + h + 1, :] for h in hs], axis=1
            )
            probs = exps[b, gi].astype(F32) * scale
            grad_prob = nt(vs[:, at], grads)
            grad_logit = (probs * (grad_prob - delta)).astype(BF16)
            dv_acc[:, at] += nn(probs.astype(BF16), grads)
            dk_acc[:, at] += nn(grad_logit, queries)
            dq = nn(kt[at, :], grad_logit)
            for c in range(chunk):
                h = gi * chunk + c
                dqp[b, h * HD : (h + 1) * HD, :] = dq[:, c * rows : (c + 1) * rows].astype(BF16)

    @pl.loop(0, n_qry)
    def _(s):
        qq = (me_q + s) % n_qry
        for j in range(r):
            b = qq * r + j
            forward(b, j)
            o, st, _ = o_args(b, j, qq)
            send(*o)
            send(*st)

        @pl.when(jnp.logical_and(s > 0, my_step == s - 1))
        def _():
            combine()

    @pl.when(my_step == n_qry - 1)
    def _():
        combine()

    @pl.loop(0, n_qry)
    def _(s):
        qq = (me_q + s) % n_qry
        for j in range(r):
            b = qq * r + j
            backward(b, j)
            send(*o_args(b, j, qq)[2])

    dk_ref[...] = (dk_acc[...] * factor).astype(BF16)
    dv_ref[...] = dv_acc[...].astype(BF16)
    for k in range(n_key):
        arrived(dqp_in.at[k], dq_r.at[k])
    for h in range(heads):
        at = slice(h * HD, (h + 1) * HD)
        total = sum(dqp_in[k, at, :].astype(F32) for k in range(n_key))
        dq_ref[:, at] = (total.T * factor).astype(BF16)

    for args in q_args + d_args + n_args:
        sent(*args)
    for q in range(n_qry):
        for j in range(r):
            for args in o_args(q * r + j, j, q):
                sent(*args)


def per_device(n_key, n_qry, queries, keys, values, out_grad):
    rows, cols = queries.shape
    key_count = keys.shape[0]
    kv_cols = keys.shape[1] // n_qry
    heads = cols // HD
    chunk = min(HQ // KVH, heads)
    ng = heads // chunk
    vmem = pl.BlockSpec(memory_space=pltpu.VMEM)
    hbm = pl.BlockSpec(memory_space=pl.ANY)
    dma = pltpu.SemaphoreType.DMA
    sems = [dma((2,))] + [dma((n_key,)) for _ in range(12)]
    return pl.pallas_call(
        functools.partial(kernel, n_key, n_qry),
        out_shape=(
            jax.ShapeDtypeStruct((rows, cols), BF16),
            jax.ShapeDtypeStruct((rows, cols), BF16),
            jax.ShapeDtypeStruct((key_count, kv_cols), BF16),
            jax.ShapeDtypeStruct((key_count, kv_cols), BF16),
        ),
        in_specs=[vmem, vmem, hbm, hbm],
        out_specs=(vmem, vmem, vmem, vmem),
        scratch_shapes=[
            pltpu.VMEM((n_key, rows, cols), BF16),
            pltpu.VMEM((n_key, rows, cols), BF16),
            pltpu.VMEM((key_count, kv_cols), BF16),
            pltpu.VMEM((key_count, kv_cols), BF16),
            pltpu.VMEM((kv_cols, key_count), BF16),
            pltpu.VMEM((kv_cols, key_count), BF16),
            pltpu.VMEM((n_key, ng, key_count, chunk * rows), BF16),
            pltpu.VMEM((n_key, cols, rows), BF16),
            pltpu.VMEM((n_key, 2 * heads, rows), F32),
            pltpu.VMEM((n_key, cols, rows), BF16),
            pltpu.VMEM((n_key, 2 * heads, rows), F32),
            pltpu.VMEM((2 * heads, rows), F32),
            pltpu.VMEM((n_key, 2 * heads, rows), F32),
            pltpu.VMEM((n_key, cols, rows), BF16),
            pltpu.VMEM((n_key, cols, rows), BF16),
            pltpu.VMEM((key_count, kv_cols), F32),
            pltpu.VMEM((key_count, kv_cols), F32),
        ]
        + sems,
        compiler_params=pltpu.CompilerParams(
            collective_id=0, has_side_effects=True, vmem_limit_bytes=60 * 1024 * 1024
        ),
        name="attention",
    )(queries, out_grad, keys, values)


def solution(mesh):
    spec_q = P(("ckpt", "qry"), "key")
    spec_k = P(("ckpt", "key"), None)
    spec_o = P(("ckpt", "key"), "qry")
    body = functools.partial(per_device, mesh.shape["key"], mesh.shape["qry"])
    return jax.shard_map(
        body,
        mesh=mesh,
        in_specs=(spec_q, spec_k, spec_k, spec_q),
        out_specs=(spec_q, spec_q, spec_o, spec_o),
        check_vma=False,
    )
```

```python
import functools
import math

import jax
import jax.numpy as jnp
from jax import lax
from jax.experimental import pallas as pl
from jax.experimental.pallas import tpu as pltpu
from jax.sharding import PartitionSpec as P

HQ = 32
KVH = 8
HD = 128
MESH = pl.DeviceIdType.MESH
F32 = jnp.float32
BF16 = jnp.bfloat16


def nt(a, b):
    return lax.dot_general(a, b, (((1,), (1,)), ((), ())), preferred_element_type=F32)


def nn(a, b):
    return lax.dot_general(a, b, (((1,), (0,)), ((), ())), preferred_element_type=F32)


def kernel(
    n_key, n_qry, split,
    q_ref, d_ref, k_hbm, v_hbm,
    attn_ref, dq_ref, dk_ref, dv_ref,
    qg, dg, ks, vs, kt, vt, exps, part, stat, part_in, stat_in, norm, norm_in,
    dqp, dqp_in, dk_acc, dv_acc, dkv, dkv_in,
    kv_sem, kx_s, kx_r, gx_s, gx_r, q_s, q_r, d_s, d_r, o_s, o_r, st_s, st_r, n_s, n_r, dq_s, dq_r,
):
    factor = 1.0 / math.sqrt(HD)
    log2e_factor = factor * math.log2(math.e)
    per_group = HQ // KVH
    r = n_key // n_qry
    nb = n_key
    rows, cols = q_ref.shape
    all_heads = cols // HD
    heads = all_heads // split
    wide = heads * HD
    chunk = min(per_group, heads)
    ng = heads // chunk
    kv_cols = ks.shape[1]
    key_count = k_hbm.shape[0]
    me_c = lax.axis_index("ckpt")
    me_k = lax.axis_index("key")
    me_q = lax.axis_index("qry")
    plane = me_k // r
    my_block = me_q * r + me_k % r
    my_step = (me_q - plane + n_qry) % n_qry

    core = me_k % split
    partner = me_k + (split - 1) - 2 * core

    def head_part(c):
        start = (me_q * split + c) * kv_cols
        return pl.ds(pl.multiple_of(start, HD), kv_cols)

    own_rows = pl.ds(pl.multiple_of(core * key_count, HD), key_count)
    k_copy = pltpu.make_async_copy(k_hbm.at[:, head_part(core)], ks.at[own_rows], kv_sem.at[0])
    v_copy = pltpu.make_async_copy(v_hbm.at[:, head_part(core)], vs.at[own_rows], kv_sem.at[1])
    k_copy.start()
    v_copy.start()

    def is_me(k, q):
        return jnp.logical_and(me_k == k, me_q == q)

    def other(k, q):
        return jnp.logical_or(me_k != k, me_q != q)

    targets = [(k, plane) for k in range(n_key)]
    sources = [(me_q * r + j, q) for q in range(n_qry) for j in range(r)]
    barrier = pltpu.get_barrier_semaphore()
    for k, q in targets + sources:
        @pl.when(other(k, q))
        def _():
            pl.semaphore_signal(barrier, inc=1, device_id=(me_c, k, q), device_id_type=MESH)

    if split > 1:
        pl.semaphore_signal(barrier, inc=1, device_id=(me_c, partner, me_q), device_id_type=MESH)

    @pl.when(plane == me_q)
    def _():
        pl.semaphore_wait(barrier, 2 * n_key - 2 + (split - 1))

    @pl.when(plane != me_q)
    def _():
        pl.semaphore_wait(barrier, 2 * n_key + (split - 1))

    def send(src, dst, ssem, rsem, k, q):
        @pl.when(is_me(k, q))
        def _():
            pltpu.make_async_copy(src, dst, rsem).start()

        @pl.when(other(k, q))
        def _():
            pltpu.make_async_remote_copy(
                src, dst, ssem, rsem, device_id=(me_c, k, q), device_id_type=MESH
            ).start()

    def sent(src, dst, ssem, rsem, k, q):
        @pl.when(other(k, q))
        def _():
            pltpu.make_async_remote_copy(
                src, dst, ssem, rsem, device_id=(me_c, k, q), device_id_type=MESH
            ).wait_send()

    def arrived(dst, rsem):
        pltpu.make_async_copy(dst, dst, rsem).wait()

    def half(k):
        return slice((k % split) * wide, (k % split + 1) * wide)

    def to_partner(src, dst, i, ssem, rsem):
        return pltpu.make_async_remote_copy(
            src, dst, ssem.at[i], rsem.at[i],
            device_id=(me_c, partner, me_q), device_id_type=MESH,
        )

    q_args = [
        (q_ref.at[:, half(k)], qg.at[my_block], q_s.at[i], q_r.at[my_block], k, q)
        for i, (k, q) in enumerate(targets)
    ]
    d_args = [
        (d_ref.at[:, half(k)], dg.at[my_block], d_s.at[i], d_r.at[my_block], k, q)
        for i, (k, q) in enumerate(targets)
    ]
    for args in q_args:
        send(*args)
    if split > 1:
        kv_moves = [
            to_partner(src.at[:, head_part(1 - core)], dst.at[own_rows], i, kx_s, kx_r)
            for i, (src, dst) in enumerate(((k_hbm, ks), (v_hbm, vs)))
        ]
        for move in kv_moves:
            move.start()
    for args in d_args:
        send(*args)

    dk_acc[...] = jnp.zeros_like(dk_acc)
    dv_acc[...] = jnp.zeros_like(dv_acc)
    k_copy.wait()
    v_copy.wait()
    if split > 1:
        for move in kv_moves:
            move.wait_recv()
    for g in range(kv_cols // HD):
        at = slice(g * HD, (g + 1) * HD)
        kt[at, :] = ks[:, at].astype(F32).T.astype(BF16)
        vt[at, :] = vs[:, at].astype(F32).T.astype(BF16)

    def stacked(ref, b, gi):
        return jnp.concatenate(
            [ref[b, :, (gi * chunk + c) * HD : (gi * chunk + c + 1) * HD] for c in range(chunk)],
            axis=0,
        )

    def o_args(b, j, qq):
        k, q = me_q * r + j, qq
        return (
            (part.at[b], part_in.at[me_k], o_s.at[b], o_r.at[me_k], k, q),
            (stat.at[b], stat_in.at[me_k], st_s.at[b], st_r.at[me_k], k, q),
            (dqp.at[b], dqp_in.at[me_k], dq_s.at[b], dq_r.at[me_k], k, q),
        )

    n_args = [
        (norm.at[k % split], norm_in.at[my_block], n_s.at[i], n_r.at[my_block], k, q)
        for i, (k, q) in enumerate(targets)
    ]

    def forward(b, j):
        arrived(qg.at[b], q_r.at[b])
        for gi in range(ng):
            kv = (j * heads + gi * chunk) // per_group
            at = slice(kv * HD, (kv + 1) * HD)
            scores = nt(ks[:, at], stacked(qg, b, gi))
            top = jnp.max(scores, axis=0, keepdims=True)
            terms = jnp.exp2(scores * log2e_factor - top * log2e_factor)
            total = jnp.sum(terms, axis=0, keepdims=True)
            small = terms.astype(BF16)
            exps[b, gi] = small
            out = nn(vt[at, :], small)
            for c in range(chunk):
                h = gi * chunk + c
                lanes = slice(c * rows, (c + 1) * rows)
                part[b, h * HD : (h + 1) * HD, :] = out[:, lanes].astype(BF16)
                stat[b, h : h + 1, :] = top[:, lanes] * factor
                stat[b, heads + h : heads + h + 1, :] = total[:, lanes]

    def combine():
        for k in range(n_key):
            arrived(part_in.at[k], o_r.at[k])
            arrived(stat_in.at[k], st_r.at[k])
        for h in range(all_heads):
            at = slice(h * HD, (h + 1) * HD)
            c, w = h // heads, h % heads
            block = slice(w * HD, (w + 1) * HD)
            members = range(c, n_key, split)
            peaks = [stat_in[k, w : w + 1, :] for k in members]
            peak = functools.reduce(jnp.maximum, peaks)
            weights = [jnp.exp(p - peak) for p in peaks]
            total = sum(
                x * stat_in[k, heads + w : heads + w + 1, :] for k, x in zip(members, weights)
            )
            out = sum(x * part_in[k, block, :].astype(F32) for k, x in zip(members, weights))
            attn = (out / total).T.astype(BF16)
            attn_ref[:, at] = attn
            product = d_ref[:, at].astype(F32) * attn.astype(F32)
            norm[c, w : w + 1, :] = peak + jnp.log(total)
            norm[c, heads + w : heads + w + 1, :] = jnp.sum(product.T, axis=0, keepdims=True)
        for args in n_args:
            send(*args)

    def backward(b, j):
        arrived(norm_in.at[b], n_r.at[b])
        arrived(dg.at[b], d_r.at[b])
        for gi in range(ng):
            kv = (j * heads + gi * chunk) // per_group
            at = slice(kv * HD, (kv + 1) * HD)
            queries = stacked(qg, b, gi)
            grads = stacked(dg, b, gi)
            hs = [gi * chunk + c for c in range(chunk)]
            scale = jnp.concatenate(
                [jnp.exp(stat[b, h : h + 1, :] - norm_in[b, h : h + 1, :]) for h in hs], axis=1
            )
            delta = jnp.concatenate(
                [norm_in[b, heads + h : heads + h + 1, :] for h in hs], axis=1
            )
            probs = exps[b, gi].astype(F32) * scale
            grad_prob = nt(vs[:, at], grads)
            grad_logit = (probs * (grad_prob - delta)).astype(BF16)
            dv_acc[:, at] += nn(probs.astype(BF16), grads)
            dk_acc[:, at] += nn(grad_logit, queries)
            dq = nn(kt[at, :], grad_logit)
            for c in range(chunk):
                h = gi * chunk + c
                dqp[b, h * HD : (h + 1) * HD, :] = dq[:, c * rows : (c + 1) * rows].astype(BF16)

    @pl.loop(0, n_qry)
    def _(s):
        qq = (me_q + s) % n_qry
        for j in range(r):
            b = qq * r + j
            forward(b, j)
            o, st, _ = o_args(b, j, qq)
            send(*o)
            send(*st)

        @pl.when(jnp.logical_and(s > 0, my_step == s - 1))
        def _():
            combine()

    @pl.when(my_step == n_qry - 1)
    def _():
        combine()

    @pl.loop(0, n_qry)
    def _(s):
        qq = (me_q + s) % n_qry
        for j in range(r):
            b = qq * r + j
            backward(b, j)
            send(*o_args(b, j, qq)[2])

    if split > 1:
        other_rows = pl.ds(pl.multiple_of((1 - core) * key_count, HD), key_count)
        dkv[0] = (dk_acc[other_rows, :] * factor).astype(BF16)
        dkv[1] = dv_acc[other_rows, :].astype(BF16)
        grad_moves = [to_partner(dkv.at[i], dkv_in.at[i], i, gx_s, gx_r) for i in range(2)]
        for move in grad_moves:
            move.start()
        for c in range(split):
            mine = slice(c * kv_cols, (c + 1) * kv_cols)

            @pl.when(core == c)
            def _():
                dk_ref[:, mine] = (dk_acc[own_rows, :] * factor).astype(BF16)
                dv_ref[:, mine] = dv_acc[own_rows, :].astype(BF16)
        for move in grad_moves:
            move.wait_recv()
        for c in range(split):
            theirs = slice((1 - c) * kv_cols, (2 - c) * kv_cols)

            @pl.when(core == c)
            def _():
                dk_ref[:, theirs] = dkv_in[0]
                dv_ref[:, theirs] = dkv_in[1]
    else:
        dk_ref[...] = (dk_acc[...] * factor).astype(BF16)
        dv_ref[...] = dv_acc[...].astype(BF16)
    for k in range(n_key):
        arrived(dqp_in.at[k], dq_r.at[k])
    for h in range(all_heads):
        at = slice(h * HD, (h + 1) * HD)
        c, w = h // heads, h % heads
        block = slice(w * HD, (w + 1) * HD)
        total = sum(dqp_in[k, block, :].astype(F32) for k in range(c, n_key, split))
        dq_ref[:, at] = (total.T * factor).astype(BF16)

    if split > 1:
        for move in kv_moves + grad_moves:
            move.wait_send()
    for args in q_args + d_args + n_args:
        sent(*args)
    for q in range(n_qry):
        for j in range(r):
            for args in o_args(q * r + j, j, q):
                sent(*args)


def per_device(n_key, n_qry, queries, keys, values, out_grad):
    rows, cols = queries.shape
    key_count = keys.shape[0]
    kv_cols = keys.shape[1] // n_qry
    split = 2 if n_key == n_qry and (kv_cols // HD) % 2 == 0 else 1
    heads = cols // HD // split
    wide = heads * HD
    chunk = min(HQ // KVH, heads)
    ng = heads // chunk
    kv_wide = kv_cols // split
    key_rows = key_count * split
    vmem = pl.BlockSpec(memory_space=pltpu.VMEM)
    hbm = pl.BlockSpec(memory_space=pl.ANY)
    dma = pltpu.SemaphoreType.DMA
    sems = [dma((2,))] + [dma((2,)) for _ in range(4)] + [dma((n_key,)) for _ in range(12)]
    return pl.pallas_call(
        functools.partial(kernel, n_key, n_qry, split),
        out_shape=(
            jax.ShapeDtypeStruct((rows, cols), BF16),
            jax.ShapeDtypeStruct((rows, cols), BF16),
            jax.ShapeDtypeStruct((key_count, kv_cols), BF16),
            jax.ShapeDtypeStruct((key_count, kv_cols), BF16),
        ),
        in_specs=[vmem, vmem, hbm, hbm],
        out_specs=(vmem, vmem, vmem, vmem),
        scratch_shapes=[
            pltpu.VMEM((n_key, rows, wide), BF16),
            pltpu.VMEM((n_key, rows, wide), BF16),
            pltpu.VMEM((key_rows, kv_wide), BF16),
            pltpu.VMEM((key_rows, kv_wide), BF16),
            pltpu.VMEM((kv_wide, key_rows), BF16),
            pltpu.VMEM((kv_wide, key_rows), BF16),
            pltpu.VMEM((n_key, ng, key_rows, chunk * rows), BF16),
            pltpu.VMEM((n_key, wide, rows), BF16),
            pltpu.VMEM((n_key, 2 * heads, rows), F32),
            pltpu.VMEM((n_key, wide, rows), BF16),
            pltpu.VMEM((n_key, 2 * heads, rows), F32),
            pltpu.VMEM((split, 2 * heads, rows), F32),
            pltpu.VMEM((n_key, 2 * heads, rows), F32),
            pltpu.VMEM((n_key, wide, rows), BF16),
            pltpu.VMEM((n_key, wide, rows), BF16),
            pltpu.VMEM((key_rows, kv_wide), F32),
            pltpu.VMEM((key_rows, kv_wide), F32),
            pltpu.VMEM((2, key_count, kv_wide), BF16),
            pltpu.VMEM((2, key_count, kv_wide), BF16),
        ]
        + sems,
        compiler_params=pltpu.CompilerParams(
            collective_id=0, has_side_effects=True, vmem_limit_bytes=60 * 1024 * 1024
        ),
        name="attention",
    )(queries, out_grad, keys, values)


def solution(mesh):
    spec_q = P(("ckpt", "qry"), "key")
    spec_k = P(("ckpt", "key"), None)
    spec_o = P(("ckpt", "key"), "qry")
    body = functools.partial(per_device, mesh.shape["key"], mesh.shape["qry"])
    return jax.shard_map(
        body,
        mesh=mesh,
        in_specs=(spec_q, spec_k, spec_k, spec_q),
        out_specs=(spec_q, spec_q, spec_o, spec_o),
        check_vma=False,
    )
```

```python
import functools
import math

import jax
import jax.numpy as jnp
from jax import lax
from jax.experimental import pallas as pl
from jax.experimental.pallas import tpu as pltpu
from jax.sharding import PartitionSpec as P

HQ = 32
KVH = 8
HD = 128
MESH = pl.DeviceIdType.MESH
F32 = jnp.float32
BF16 = jnp.bfloat16


def nt(a, b):
    return lax.dot_general(a, b, (((1,), (1,)), ((), ())), preferred_element_type=F32)


def nn(a, b):
    return lax.dot_general(a, b, (((1,), (0,)), ((), ())), preferred_element_type=F32)


def kernel(
    n_key, n_qry, split, relay,
    q_ref, d_ref, k_hbm, v_hbm,
    attn_ref, dq_ref, dk_ref, dv_ref,
    qg, dg, ks, vs, kt, vt, exps, part, stat, part_in, stat_in, norm, norm_in,
    dqp, dqp_in, dk_acc, dv_acc, dkv, dkv_in, crossed,
    kv_sem, kx_s, kx_r, gx_s, gx_r, q_s, q_r, d_s, d_r, o_s, o_r, st_s, st_r, n_s, n_r, dq_s, dq_r, q_xs, q_xr, d_xs, d_xr, x_s, x_r,
):
    factor = 1.0 / math.sqrt(HD)
    log2e_factor = factor * math.log2(math.e)
    per_group = HQ // KVH
    r = n_key // n_qry
    nb = n_key
    rows, cols = q_ref.shape
    all_heads = cols // HD
    heads = all_heads // split
    wide = heads * HD
    chunk = min(per_group, heads)
    ng = heads // chunk
    kv_cols = ks.shape[1]
    key_count = k_hbm.shape[0]
    me_c = lax.axis_index("ckpt")
    me_k = lax.axis_index("key")
    me_q = lax.axis_index("qry")
    plane = me_k // r
    my_block = me_q * r + me_k % r
    my_step = (me_q - plane + n_qry) % n_qry

    core = me_k % split
    partner = me_k + (split - 1) - 2 * core

    def head_part(c):
        start = (me_q * split + c) * kv_cols
        return pl.ds(pl.multiple_of(start, HD), kv_cols)

    own_rows = pl.ds(pl.multiple_of(core * key_count, HD), key_count)
    k_copy = pltpu.make_async_copy(k_hbm.at[:, head_part(core)], ks.at[own_rows], kv_sem.at[0])
    v_copy = pltpu.make_async_copy(v_hbm.at[:, head_part(core)], vs.at[own_rows], kv_sem.at[1])
    k_copy.start()
    v_copy.start()

    def is_me(k, q):
        return jnp.logical_and(me_k == k, me_q == q)

    def other(k, q):
        return jnp.logical_or(me_k != k, me_q != q)

    targets = [(k, plane) for k in range(n_key)]
    sources = [(me_q * r + j, q) for q in range(n_qry) for j in range(r)]
    barrier = pltpu.get_barrier_semaphore()
    if relay:
        for k in range(n_key):
            for q in range(n_qry):
                @pl.when(other(k, q))
                def _():
                    pl.semaphore_signal(
                        barrier, inc=1, device_id=(me_c, k, q), device_id_type=MESH
                    )

        pl.semaphore_wait(barrier, n_key * n_qry - 1)
    else:
        for k, q in targets + sources:
            @pl.when(other(k, q))
            def _():
                pl.semaphore_signal(barrier, inc=1, device_id=(me_c, k, q), device_id_type=MESH)

        if split > 1:
            pl.semaphore_signal(barrier, inc=1, device_id=(me_c, partner, me_q), device_id_type=MESH)

        @pl.when(plane == me_q)
        def _():
            pl.semaphore_wait(barrier, 2 * n_key - 2 + (split - 1))

        @pl.when(plane != me_q)
        def _():
            pl.semaphore_wait(barrier, 2 * n_key + (split - 1))

    def send(src, dst, ssem, rsem, k, q):
        @pl.when(is_me(k, q))
        def _():
            pltpu.make_async_copy(src, dst, rsem).start()

        @pl.when(other(k, q))
        def _():
            pltpu.make_async_remote_copy(
                src, dst, ssem, rsem, device_id=(me_c, k, q), device_id_type=MESH
            ).start()

    def sent(src, dst, ssem, rsem, k, q):
        @pl.when(other(k, q))
        def _():
            pltpu.make_async_remote_copy(
                src, dst, ssem, rsem, device_id=(me_c, k, q), device_id_type=MESH
            ).wait_send()

    def arrived(dst, rsem):
        pltpu.make_async_copy(dst, dst, rsem).wait()

    def half(k):
        return slice((k % split) * wide, (k % split + 1) * wide)

    def to_partner(src, dst, i, ssem, rsem):
        return pltpu.make_async_remote_copy(
            src, dst, ssem.at[i], rsem.at[i],
            device_id=(me_c, partner, me_q), device_id_type=MESH,
        )

    q_args = [
        (q_ref.at[:, half(k)], qg.at[my_block], q_s.at[i], q_r.at[my_block], k, q)
        for i, (k, q) in enumerate(targets)
    ]
    d_args = [
        (d_ref.at[:, half(k)], dg.at[my_block], d_s.at[i], d_r.at[my_block], k, q)
        for i, (k, q) in enumerate(targets)
    ]
    if split > 1:
        kv_moves = [
            to_partner(src.at[:, head_part(1 - core)], dst.at[own_rows], i, kx_s, kx_r)
            for i, (src, dst) in enumerate(((k_hbm, ks), (v_hbm, vs)))
        ]
    if relay:
        low = rows // 2
        chip = me_k // split
        beside = (1 - chip) * split + core
        far = (chip + me_q // split) % 2
        got = pl.ds(pl.multiple_of(far * low, low), low)

        def across(src, dst, ssem, rsem):
            return pltpu.make_async_remote_copy(
                src, dst, ssem, rsem, device_id=(me_c, beside, me_q), device_id_type=MESH
            )

        crossing = [
            across(ref.at[low:rows], crossed.at[i], x_s.at[i], x_r.at[i])
            for i, ref in enumerate((q_ref, d_ref))
        ]

        def along(ref, gathered, ssem, rsem, i):
            near = [
                (ref.at[0:low, half(c)], gathered.at[me_q, 0:low], ssem.at[c], rsem.at[me_q],
                 chip * split + c, me_k)
                for c in range(split)
            ]
            turned = [
                (crossed.at[i, :, half(c)], gathered.at[me_q, low:rows], ssem.at[split + c],
                 rsem.at[me_q], chip * split + c, beside)
                for c in range(split)
            ]
            return near, turned

        def passed(gathered, ssem, rsem, b):
            return across(gathered.at[b, got], gathered.at[b, got], ssem.at[b], rsem.at[b])

        q_near, q_turned = along(q_ref, qg, q_s, q_r, 0)
        d_near, d_turned = along(d_ref, dg, d_s, d_r, 1)
        q_args, d_args = q_near + q_turned, d_near + d_turned
        for move in crossing:
            move.start()
        for args in q_near:
            send(*args)
        for move in kv_moves:
            move.start()
        crossing[0].wait_recv()
        for args in q_turned + d_near:
            send(*args)
        crossing[1].wait_recv()
        for args in d_turned:
            send(*args)
    else:
        for args in q_args:
            send(*args)
        if split > 1:
            for move in kv_moves:
                move.start()
        for args in d_args:
            send(*args)

    dk_acc[...] = jnp.zeros_like(dk_acc)
    dv_acc[...] = jnp.zeros_like(dv_acc)
    k_copy.wait()
    v_copy.wait()
    if split > 1:
        for move in kv_moves:
            move.wait_recv()
    for g in range(kv_cols // HD):
        at = slice(g * HD, (g + 1) * HD)
        kt[at, :] = ks[:, at].astype(F32).T.astype(BF16)
        vt[at, :] = vs[:, at].astype(F32).T.astype(BF16)

    if relay:
        for i in range(n_qry):
            b = (me_q + i) % n_qry
            arrived(qg.at[b, got], q_r.at[b])
            passed(qg, q_xs, q_xr, b).start()

    def stacked(ref, b, gi):
        return jnp.concatenate(
            [ref[b, :, (gi * chunk + c) * HD : (gi * chunk + c + 1) * HD] for c in range(chunk)],
            axis=0,
        )

    def o_args(b, j, qq):
        k, q = me_q * r + j, qq
        return (
            (part.at[b], part_in.at[me_k], o_s.at[b], o_r.at[me_k], k, q),
            (stat.at[b], stat_in.at[me_k], st_s.at[b], st_r.at[me_k], k, q),
            (dqp.at[b], dqp_in.at[me_k], dq_s.at[b], dq_r.at[me_k], k, q),
        )

    n_args = [
        (norm.at[k % split], norm_in.at[my_block], n_s.at[i], n_r.at[my_block], k, q)
        for i, (k, q) in enumerate(targets)
    ]

    def forward(b, j):
        if relay:
            passed(qg, q_xs, q_xr, b).wait_recv()
        else:
            arrived(qg.at[b], q_r.at[b])
        for gi in range(ng):
            kv = (j * heads + gi * chunk) // per_group
            at = slice(kv * HD, (kv + 1) * HD)
            scores = nt(ks[:, at], stacked(qg, b, gi))
            top = jnp.max(scores, axis=0, keepdims=True)
            terms = jnp.exp2(scores * log2e_factor - top * log2e_factor)
            total = jnp.sum(terms, axis=0, keepdims=True)
            small = terms.astype(BF16)
            exps[b, gi] = small
            out = nn(vt[at, :], small)
            for c in range(chunk):
                h = gi * chunk + c
                lanes = slice(c * rows, (c + 1) * rows)
                part[b, h * HD : (h + 1) * HD, :] = out[:, lanes].astype(BF16)
                stat[b, h : h + 1, :] = top[:, lanes] * factor
                stat[b, heads + h : heads + h + 1, :] = total[:, lanes]

    def combine():
        for k in range(n_key):
            arrived(part_in.at[k], o_r.at[k])
            arrived(stat_in.at[k], st_r.at[k])
        for h in range(all_heads):
            at = slice(h * HD, (h + 1) * HD)
            c, w = h // heads, h % heads
            block = slice(w * HD, (w + 1) * HD)
            members = range(c, n_key, split)
            peaks = [stat_in[k, w : w + 1, :] for k in members]
            peak = functools.reduce(jnp.maximum, peaks)
            weights = [jnp.exp(p - peak) for p in peaks]
            total = sum(
                x * stat_in[k, heads + w : heads + w + 1, :] for k, x in zip(members, weights)
            )
            out = sum(x * part_in[k, block, :].astype(F32) for k, x in zip(members, weights))
            attn = (out / total).T.astype(BF16)
            attn_ref[:, at] = attn
            product = d_ref[:, at].astype(F32) * attn.astype(F32)
            norm[c, w : w + 1, :] = peak + jnp.log(total)
            norm[c, heads + w : heads + w + 1, :] = jnp.sum(product.T, axis=0, keepdims=True)
        for args in n_args:
            send(*args)

    def backward(b, j):
        arrived(norm_in.at[b], n_r.at[b])
        if relay:
            passed(dg, d_xs, d_xr, b).wait_recv()
        else:
            arrived(dg.at[b], d_r.at[b])
        for gi in range(ng):
            kv = (j * heads + gi * chunk) // per_group
            at = slice(kv * HD, (kv + 1) * HD)
            queries = stacked(qg, b, gi)
            grads = stacked(dg, b, gi)
            hs = [gi * chunk + c for c in range(chunk)]
            scale = jnp.concatenate(
                [jnp.exp(stat[b, h : h + 1, :] - norm_in[b, h : h + 1, :]) for h in hs], axis=1
            )
            delta = jnp.concatenate(
                [norm_in[b, heads + h : heads + h + 1, :] for h in hs], axis=1
            )
            probs = exps[b, gi].astype(F32) * scale
            grad_prob = nt(vs[:, at], grads)
            grad_logit = (probs * (grad_prob - delta)).astype(BF16)
            dv_acc[:, at] += nn(probs.astype(BF16), grads)
            dk_acc[:, at] += nn(grad_logit, queries)
            dq = nn(kt[at, :], grad_logit)
            for c in range(chunk):
                h = gi * chunk + c
                dqp[b, h * HD : (h + 1) * HD, :] = dq[:, c * rows : (c + 1) * rows].astype(BF16)

    @pl.loop(0, n_qry)
    def _(s):
        qq = (me_q + s) % n_qry
        for j in range(r):
            b = qq * r + j
            forward(b, j)
            o, st, _ = o_args(b, j, qq)
            send(*o)
            send(*st)
            if relay:
                arrived(dg.at[b, got], d_r.at[b])
                passed(dg, d_xs, d_xr, b).start()

        @pl.when(jnp.logical_and(s > 0, my_step == s - 1))
        def _():
            combine()

    @pl.when(my_step == n_qry - 1)
    def _():
        combine()

    @pl.loop(0, n_qry)
    def _(s):
        qq = (me_q + s) % n_qry
        for j in range(r):
            b = qq * r + j
            backward(b, j)
            send(*o_args(b, j, qq)[2])

    if split > 1:
        other_rows = pl.ds(pl.multiple_of((1 - core) * key_count, HD), key_count)
        dkv[0] = (dk_acc[other_rows, :] * factor).astype(BF16)
        dkv[1] = dv_acc[other_rows, :].astype(BF16)
        grad_moves = [to_partner(dkv.at[i], dkv_in.at[i], i, gx_s, gx_r) for i in range(2)]
        for move in grad_moves:
            move.start()
        for c in range(split):
            mine = slice(c * kv_cols, (c + 1) * kv_cols)

            @pl.when(core == c)
            def _():
                dk_ref[:, mine] = (dk_acc[own_rows, :] * factor).astype(BF16)
                dv_ref[:, mine] = dv_acc[own_rows, :].astype(BF16)
        for move in grad_moves:
            move.wait_recv()
        for c in range(split):
            theirs = slice((1 - c) * kv_cols, (2 - c) * kv_cols)

            @pl.when(core == c)
            def _():
                dk_ref[:, theirs] = dkv_in[0]
                dv_ref[:, theirs] = dkv_in[1]
    else:
        dk_ref[...] = (dk_acc[...] * factor).astype(BF16)
        dv_ref[...] = dv_acc[...].astype(BF16)
    for k in range(n_key):
        arrived(dqp_in.at[k], dq_r.at[k])
    for h in range(all_heads):
        at = slice(h * HD, (h + 1) * HD)
        c, w = h // heads, h % heads
        block = slice(w * HD, (w + 1) * HD)
        total = sum(dqp_in[k, block, :].astype(F32) for k in range(c, n_key, split))
        dq_ref[:, at] = (total.T * factor).astype(BF16)

    if split > 1:
        for move in kv_moves + grad_moves:
            move.wait_send()
    if relay:
        for move in crossing:
            move.wait_send()
        for b in range(n_qry):
            passed(qg, q_xs, q_xr, b).wait_send()
            passed(dg, d_xs, d_xr, b).wait_send()
    for args in q_args + d_args + n_args:
        sent(*args)
    for q in range(n_qry):
        for j in range(r):
            for args in o_args(q * r + j, j, q):
                sent(*args)


def per_device(n_key, n_qry, queries, keys, values, out_grad):
    rows, cols = queries.shape
    key_count = keys.shape[0]
    kv_cols = keys.shape[1] // n_qry
    split = 2 if n_key == n_qry and (kv_cols // HD) % 2 == 0 else 1
    relay = split == 2 and n_key == 2 * split and rows % 32 == 0
    heads = cols // HD // split
    wide = heads * HD
    chunk = min(HQ // KVH, heads)
    ng = heads // chunk
    kv_wide = kv_cols // split
    key_rows = key_count * split
    vmem = pl.BlockSpec(memory_space=pltpu.VMEM)
    hbm = pl.BlockSpec(memory_space=pl.ANY)
    dma = pltpu.SemaphoreType.DMA
    sems = [dma((2,))] + [dma((2,)) for _ in range(4)] + [dma((n_key,)) for _ in range(16)]
    sems.append(dma((2,)))
    sems.append(dma((2,)))
    return pl.pallas_call(
        functools.partial(kernel, n_key, n_qry, split, relay),
        out_shape=(
            jax.ShapeDtypeStruct((rows, cols), BF16),
            jax.ShapeDtypeStruct((rows, cols), BF16),
            jax.ShapeDtypeStruct((key_count, kv_cols), BF16),
            jax.ShapeDtypeStruct((key_count, kv_cols), BF16),
        ),
        in_specs=[vmem, vmem, hbm, hbm],
        out_specs=(vmem, vmem, vmem, vmem),
        scratch_shapes=[
            pltpu.VMEM((n_key, rows, wide), BF16),
            pltpu.VMEM((n_key, rows, wide), BF16),
            pltpu.VMEM((key_rows, kv_wide), BF16),
            pltpu.VMEM((key_rows, kv_wide), BF16),
            pltpu.VMEM((kv_wide, key_rows), BF16),
            pltpu.VMEM((kv_wide, key_rows), BF16),
            pltpu.VMEM((n_key, ng, key_rows, chunk * rows), BF16),
            pltpu.VMEM((n_key, wide, rows), BF16),
            pltpu.VMEM((n_key, 2 * heads, rows), F32),
            pltpu.VMEM((n_key, wide, rows), BF16),
            pltpu.VMEM((n_key, 2 * heads, rows), F32),
            pltpu.VMEM((split, 2 * heads, rows), F32),
            pltpu.VMEM((n_key, 2 * heads, rows), F32),
            pltpu.VMEM((n_key, wide, rows), BF16),
            pltpu.VMEM((n_key, wide, rows), BF16),
            pltpu.VMEM((key_rows, kv_wide), F32),
            pltpu.VMEM((key_rows, kv_wide), F32),
            pltpu.VMEM((2, key_count, kv_wide), BF16),
            pltpu.VMEM((2, key_count, kv_wide), BF16),
            pltpu.VMEM((2, rows // 2, cols), BF16),
        ]
        + sems,
        compiler_params=pltpu.CompilerParams(
            collective_id=0, has_side_effects=True, vmem_limit_bytes=60 * 1024 * 1024
        ),
        name="attention",
    )(queries, out_grad, keys, values)


def solution(mesh):
    spec_q = P(("ckpt", "qry"), "key")
    spec_k = P(("ckpt", "key"), None)
    spec_o = P(("ckpt", "key"), "qry")
    body = functools.partial(per_device, mesh.shape["key"], mesh.shape["qry"])
    return jax.shard_map(
        body,
        mesh=mesh,
        in_specs=(spec_q, spec_k, spec_k, spec_q),
        out_specs=(spec_q, spec_q, spec_o, spec_o),
        check_vma=False,
    )
```

```python
import functools
import math

import jax
import jax.numpy as jnp
from jax import lax
from jax.experimental import pallas as pl
from jax.experimental.pallas import tpu as pltpu
from jax.sharding import PartitionSpec as P

HQ = 32
KVH = 8
HD = 128
MESH = pl.DeviceIdType.MESH
F32 = jnp.float32
BF16 = jnp.bfloat16


def nt(a, b):
    return lax.dot_general(a, b, (((1,), (1,)), ((), ())), preferred_element_type=F32)


def nn(a, b):
    return lax.dot_general(a, b, (((1,), (0,)), ((), ())), preferred_element_type=F32)


def kernel(
    n_key, n_qry, split, relay,
    q_ref, d_ref, k_hbm, v_hbm,
    attn_ref, dq_ref, dk_ref, dv_ref,
    qg, dg, ks, vs, kt, vt, exps, part, stat, part_in, stat_in, norm, norm_in,
    dqp, dqp_in, dk_acc, dv_acc, dkv, dkv_in, crossed,
    kv_sem, kx_s, kx_r, gx_s, gx_r, q_s, q_r, d_s, d_r, o_s, o_r, st_s, st_r, n_s, n_r, dq_s, dq_r, q_xs, q_xr, d_xs, d_xr, x_s, x_r,
):
    factor = 1.0 / math.sqrt(HD)
    log2e_factor = factor * math.log2(math.e)
    per_group = HQ // KVH
    r = n_key // n_qry
    nb = n_key
    rows, cols = q_ref.shape
    all_heads = cols // HD
    heads = all_heads // split
    wide = heads * HD
    chunk = min(per_group, heads)
    ng = heads // chunk
    kv_cols = ks.shape[1]
    key_count = k_hbm.shape[0]
    me_c = lax.axis_index("ckpt")
    me_k = lax.axis_index("key")
    me_q = lax.axis_index("qry")
    plane = me_k // r
    my_block = me_q * r + me_k % r
    my_step = (me_q - plane + n_qry) % n_qry

    core = me_k % split
    partner = me_k + (split - 1) - 2 * core

    def head_part(c):
        start = (me_q * split + c) * kv_cols
        return pl.ds(pl.multiple_of(start, HD), kv_cols)

    own_rows = pl.ds(pl.multiple_of(core * key_count, HD), key_count)
    k_copy = pltpu.make_async_copy(k_hbm.at[:, head_part(core)], ks.at[own_rows], kv_sem.at[0])
    v_copy = pltpu.make_async_copy(v_hbm.at[:, head_part(core)], vs.at[own_rows], kv_sem.at[1])
    k_copy.start()
    v_copy.start()

    def is_me(k, q):
        return jnp.logical_and(me_k == k, me_q == q)

    def other(k, q):
        return jnp.logical_or(me_k != k, me_q != q)

    targets = [(k, plane) for k in range(n_key)]
    sources = [(me_q * r + j, q) for q in range(n_qry) for j in range(r)]
    barrier = pltpu.get_barrier_semaphore()
    if relay:
        for k in range(n_key):
            for q in range(n_qry):
                @pl.when(other(k, q))
                def _():
                    pl.semaphore_signal(
                        barrier, inc=1, device_id=(me_c, k, q), device_id_type=MESH
                    )

        pl.semaphore_wait(barrier, n_key * n_qry - 1)
    else:
        for k, q in targets + sources:
            @pl.when(other(k, q))
            def _():
                pl.semaphore_signal(barrier, inc=1, device_id=(me_c, k, q), device_id_type=MESH)

        if split > 1:
            pl.semaphore_signal(barrier, inc=1, device_id=(me_c, partner, me_q), device_id_type=MESH)

        @pl.when(plane == me_q)
        def _():
            pl.semaphore_wait(barrier, 2 * n_key - 2 + (split - 1))

        @pl.when(plane != me_q)
        def _():
            pl.semaphore_wait(barrier, 2 * n_key + (split - 1))

    def send(src, dst, ssem, rsem, k, q):
        @pl.when(is_me(k, q))
        def _():
            pltpu.make_async_copy(src, dst, rsem).start()

        @pl.when(other(k, q))
        def _():
            pltpu.make_async_remote_copy(
                src, dst, ssem, rsem, device_id=(me_c, k, q), device_id_type=MESH
            ).start()

    def sent(src, dst, ssem, rsem, k, q):
        @pl.when(other(k, q))
        def _():
            pltpu.make_async_remote_copy(
                src, dst, ssem, rsem, device_id=(me_c, k, q), device_id_type=MESH
            ).wait_send()

    def arrived(dst, rsem):
        pltpu.make_async_copy(dst, dst, rsem).wait()

    def half(k):
        return slice((k % split) * wide, (k % split + 1) * wide)

    def to_partner(src, dst, i, ssem, rsem):
        return pltpu.make_async_remote_copy(
            src, dst, ssem.at[i], rsem.at[i],
            device_id=(me_c, partner, me_q), device_id_type=MESH,
        )

    q_args = [
        (q_ref.at[:, half(k)], qg.at[my_block], q_s.at[i], q_r.at[my_block], k, q)
        for i, (k, q) in enumerate(targets)
    ]
    d_args = [
        (d_ref.at[:, half(k)], dg.at[my_block], d_s.at[i], d_r.at[my_block], k, q)
        for i, (k, q) in enumerate(targets)
    ]
    if split > 1:
        kv_moves = [
            to_partner(src.at[:, head_part(1 - core)], dst.at[own_rows], i, kx_s, kx_r)
            for i, (src, dst) in enumerate(((k_hbm, ks), (v_hbm, vs)))
        ]
    if relay:
        low = rows // 2
        chip = me_k // split
        beside = (1 - chip) * split + core
        far = (chip + me_q // split) % 2
        got = pl.ds(pl.multiple_of(far * low, low), low)

        def across(src, dst, ssem, rsem):
            return pltpu.make_async_remote_copy(
                src, dst, ssem, rsem, device_id=(me_c, beside, me_q), device_id_type=MESH
            )

        crossing = [
            across(ref.at[low:rows], crossed.at[i], x_s.at[i], x_r.at[i])
            for i, ref in enumerate((q_ref, d_ref))
        ]

        def along(ref, gathered, ssem, rsem, i):
            near = [
                (ref.at[0:low, half(c)], gathered.at[me_q, 0:low], ssem.at[c], rsem.at[me_q],
                 chip * split + c, me_k)
                for c in range(split)
            ]
            turned = [
                (crossed.at[i, :, half(c)], gathered.at[me_q, low:rows], ssem.at[split + c],
                 rsem.at[me_q], chip * split + c, beside)
                for c in range(split)
            ]
            return near, turned

        def passed(gathered, ssem, rsem, b):
            return across(gathered.at[b, got], gathered.at[b, got], ssem.at[b], rsem.at[b])

        q_near, q_turned = along(q_ref, qg, q_s, q_r, 0)
        d_near, d_turned = along(d_ref, dg, d_s, d_r, 1)
        q_args, d_args = q_near + q_turned, d_near + d_turned
        for move in crossing:
            move.start()
        for args in q_near:
            send(*args)
        for move in kv_moves:
            move.start()
        crossing[0].wait_recv()
        for args in q_turned + d_near:
            send(*args)
        crossing[1].wait_recv()
        for args in d_turned:
            send(*args)
    else:
        for args in q_args:
            send(*args)
        if split > 1:
            for move in kv_moves:
                move.start()
        for args in d_args:
            send(*args)

    dk_acc[...] = jnp.zeros_like(dk_acc)
    dv_acc[...] = jnp.zeros_like(dv_acc)
    k_copy.wait()
    v_copy.wait()
    if split > 1:
        for move in kv_moves:
            move.wait_recv()
    for g in range(kv_cols // HD):
        at = slice(g * HD, (g + 1) * HD)
        kt[at, :] = ks[:, at].astype(F32).T.astype(BF16)
        vt[at, :] = vs[:, at].astype(F32).T.astype(BF16)

    ahead = min(2, n_qry)

    def pass_queries(b):
        arrived(qg.at[b, got], q_r.at[b])
        passed(qg, q_xs, q_xr, b).start()

    if relay:
        for i in range(ahead):
            pass_queries((me_q + i) % n_qry)

    def stacked(ref, b, gi):
        return jnp.concatenate(
            [ref[b, :, (gi * chunk + c) * HD : (gi * chunk + c + 1) * HD] for c in range(chunk)],
            axis=0,
        )

    def o_args(b, j, qq):
        k, q = me_q * r + j, qq
        return (
            (part.at[b], part_in.at[me_k], o_s.at[b], o_r.at[me_k], k, q),
            (stat.at[b], stat_in.at[me_k], st_s.at[b], st_r.at[me_k], k, q),
            (dqp.at[b], dqp_in.at[me_k], dq_s.at[b], dq_r.at[me_k], k, q),
        )

    n_args = [
        (norm.at[k % split], norm_in.at[my_block], n_s.at[i], n_r.at[my_block], k, q)
        for i, (k, q) in enumerate(targets)
    ]

    def forward(b, j):
        if relay:
            passed(qg, q_xs, q_xr, b).wait_recv()
        else:
            arrived(qg.at[b], q_r.at[b])
        for gi in range(ng):
            kv = (j * heads + gi * chunk) // per_group
            at = slice(kv * HD, (kv + 1) * HD)
            scores = nt(ks[:, at], stacked(qg, b, gi))
            top = jnp.max(scores, axis=0, keepdims=True)
            terms = jnp.exp2(scores * log2e_factor - top * log2e_factor)
            total = jnp.sum(terms, axis=0, keepdims=True)
            small = terms.astype(BF16)
            exps[b, gi] = small
            out = nn(vt[at, :], small)
            for c in range(chunk):
                h = gi * chunk + c
                lanes = slice(c * rows, (c + 1) * rows)
                part[b, h * HD : (h + 1) * HD, :] = out[:, lanes].astype(BF16)
                stat[b, h : h + 1, :] = top[:, lanes] * factor
                stat[b, heads + h : heads + h + 1, :] = total[:, lanes]

    def combine():
        for k in range(n_key):
            arrived(part_in.at[k], o_r.at[k])
            arrived(stat_in.at[k], st_r.at[k])
        for h in range(all_heads):
            at = slice(h * HD, (h + 1) * HD)
            c, w = h // heads, h % heads
            block = slice(w * HD, (w + 1) * HD)
            members = range(c, n_key, split)
            peaks = [stat_in[k, w : w + 1, :] for k in members]
            peak = functools.reduce(jnp.maximum, peaks)
            weights = [jnp.exp(p - peak) for p in peaks]
            total = sum(
                x * stat_in[k, heads + w : heads + w + 1, :] for k, x in zip(members, weights)
            )
            out = sum(x * part_in[k, block, :].astype(F32) for k, x in zip(members, weights))
            attn = (out / total).T.astype(BF16)
            attn_ref[:, at] = attn
            product = d_ref[:, at].astype(F32) * attn.astype(F32)
            norm[c, w : w + 1, :] = peak + jnp.log(total)
            norm[c, heads + w : heads + w + 1, :] = jnp.sum(product.T, axis=0, keepdims=True)
        for args in n_args:
            send(*args)

    def backward(b, j):
        arrived(norm_in.at[b], n_r.at[b])
        if relay:
            passed(dg, d_xs, d_xr, b).wait_recv()
        else:
            arrived(dg.at[b], d_r.at[b])
        for gi in range(ng):
            kv = (j * heads + gi * chunk) // per_group
            at = slice(kv * HD, (kv + 1) * HD)
            queries = stacked(qg, b, gi)
            grads = stacked(dg, b, gi)
            hs = [gi * chunk + c for c in range(chunk)]
            scale = jnp.concatenate(
                [jnp.exp(stat[b, h : h + 1, :] - norm_in[b, h : h + 1, :]) for h in hs], axis=1
            )
            delta = jnp.concatenate(
                [norm_in[b, heads + h : heads + h + 1, :] for h in hs], axis=1
            )
            probs = exps[b, gi].astype(F32) * scale
            grad_prob = nt(vs[:, at], grads)
            grad_logit = (probs * (grad_prob - delta)).astype(BF16)
            dv_acc[:, at] += nn(probs.astype(BF16), grads)
            dk_acc[:, at] += nn(grad_logit, queries)
            dq = nn(kt[at, :], grad_logit)
            for c in range(chunk):
                h = gi * chunk + c
                dqp[b, h * HD : (h + 1) * HD, :] = dq[:, c * rows : (c + 1) * rows].astype(BF16)

    @pl.loop(0, n_qry)
    def _(s):
        qq = (me_q + s) % n_qry
        for j in range(r):
            b = qq * r + j
            forward(b, j)
            o, st, _ = o_args(b, j, qq)
            send(*o)
            send(*st)
            if relay:
                @pl.when(s + ahead < n_qry)
                def _():
                    pass_queries((me_q + s + ahead) % n_qry)

                arrived(dg.at[b, got], d_r.at[b])
                passed(dg, d_xs, d_xr, b).start()

        @pl.when(jnp.logical_and(s > 0, my_step == s - 1))
        def _():
            combine()

    @pl.when(my_step == n_qry - 1)
    def _():
        combine()

    @pl.loop(0, n_qry)
    def _(s):
        qq = (me_q + s + 1) % n_qry
        for j in range(r):
            b = qq * r + j
            backward(b, j)
            send(*o_args(b, j, qq)[2])

    if split > 1:
        other_rows = pl.ds(pl.multiple_of((1 - core) * key_count, HD), key_count)
        dkv[0] = (dk_acc[other_rows, :] * factor).astype(BF16)
        dkv[1] = dv_acc[other_rows, :].astype(BF16)
        grad_moves = [to_partner(dkv.at[i], dkv_in.at[i], i, gx_s, gx_r) for i in range(2)]
        for move in grad_moves:
            move.start()
        for c in range(split):
            mine = slice(c * kv_cols, (c + 1) * kv_cols)

            @pl.when(core == c)
            def _():
                dk_ref[:, mine] = (dk_acc[own_rows, :] * factor).astype(BF16)
                dv_ref[:, mine] = dv_acc[own_rows, :].astype(BF16)
        for move in grad_moves:
            move.wait_recv()
        for c in range(split):
            theirs = slice((1 - c) * kv_cols, (2 - c) * kv_cols)

            @pl.when(core == c)
            def _():
                dk_ref[:, theirs] = dkv_in[0]
                dv_ref[:, theirs] = dkv_in[1]
    else:
        dk_ref[...] = (dk_acc[...] * factor).astype(BF16)
        dv_ref[...] = dv_acc[...].astype(BF16)
    for k in range(n_key):
        arrived(dqp_in.at[k], dq_r.at[k])
    for h in range(all_heads):
        at = slice(h * HD, (h + 1) * HD)
        c, w = h // heads, h % heads
        block = slice(w * HD, (w + 1) * HD)
        total = sum(dqp_in[k, block, :].astype(F32) for k in range(c, n_key, split))
        dq_ref[:, at] = (total.T * factor).astype(BF16)

    if split > 1:
        for move in kv_moves + grad_moves:
            move.wait_send()
    if relay:
        for move in crossing:
            move.wait_send()
        for b in range(n_qry):
            passed(qg, q_xs, q_xr, b).wait_send()
            passed(dg, d_xs, d_xr, b).wait_send()
    for args in q_args + d_args + n_args:
        sent(*args)
    for q in range(n_qry):
        for j in range(r):
            for args in o_args(q * r + j, j, q):
                sent(*args)


def per_device(n_key, n_qry, queries, keys, values, out_grad):
    rows, cols = queries.shape
    key_count = keys.shape[0]
    kv_cols = keys.shape[1] // n_qry
    split = 2 if n_key == n_qry and (kv_cols // HD) % 2 == 0 else 1
    relay = split == 2 and n_key == 2 * split and rows % 32 == 0
    heads = cols // HD // split
    wide = heads * HD
    chunk = min(HQ // KVH, heads)
    ng = heads // chunk
    kv_wide = kv_cols // split
    key_rows = key_count * split
    vmem = pl.BlockSpec(memory_space=pltpu.VMEM)
    hbm = pl.BlockSpec(memory_space=pl.ANY)
    dma = pltpu.SemaphoreType.DMA
    sems = [dma((2,))] + [dma((2,)) for _ in range(4)] + [dma((n_key,)) for _ in range(16)]
    sems.append(dma((2,)))
    sems.append(dma((2,)))
    return pl.pallas_call(
        functools.partial(kernel, n_key, n_qry, split, relay),
        out_shape=(
            jax.ShapeDtypeStruct((rows, cols), BF16),
            jax.ShapeDtypeStruct((rows, cols), BF16),
            jax.ShapeDtypeStruct((key_count, kv_cols), BF16),
            jax.ShapeDtypeStruct((key_count, kv_cols), BF16),
        ),
        in_specs=[vmem, vmem, hbm, hbm],
        out_specs=(vmem, vmem, vmem, vmem),
        scratch_shapes=[
            pltpu.VMEM((n_key, rows, wide), BF16),
            pltpu.VMEM((n_key, rows, wide), BF16),
            pltpu.VMEM((key_rows, kv_wide), BF16),
            pltpu.VMEM((key_rows, kv_wide), BF16),
            pltpu.VMEM((kv_wide, key_rows), BF16),
            pltpu.VMEM((kv_wide, key_rows), BF16),
            pltpu.VMEM((n_key, ng, key_rows, chunk * rows), BF16),
            pltpu.VMEM((n_key, wide, rows), BF16),
            pltpu.VMEM((n_key, 2 * heads, rows), F32),
            pltpu.VMEM((n_key, wide, rows), BF16),
            pltpu.VMEM((n_key, 2 * heads, rows), F32),
            pltpu.VMEM((split, 2 * heads, rows), F32),
            pltpu.VMEM((n_key, 2 * heads, rows), F32),
            pltpu.VMEM((n_key, wide, rows), BF16),
            pltpu.VMEM((n_key, wide, rows), BF16),
            pltpu.VMEM((key_rows, kv_wide), F32),
            pltpu.VMEM((key_rows, kv_wide), F32),
            pltpu.VMEM((2, key_count, kv_wide), BF16),
            pltpu.VMEM((2, key_count, kv_wide), BF16),
            pltpu.VMEM((2, rows // 2, cols), BF16),
        ]
        + sems,
        compiler_params=pltpu.CompilerParams(
            collective_id=0, has_side_effects=True, vmem_limit_bytes=60 * 1024 * 1024
        ),
        name="attention",
    )(queries, out_grad, keys, values)


def solution(mesh):
    spec_q = P(("ckpt", "qry"), "key")
    spec_k = P(("ckpt", "key"), None)
    spec_o = P(("ckpt", "key"), "qry")
    body = functools.partial(per_device, mesh.shape["key"], mesh.shape["qry"])
    return jax.shard_map(
        body,
        mesh=mesh,
        in_specs=(spec_q, spec_k, spec_k, spec_q),
        out_specs=(spec_q, spec_q, spec_o, spec_o),
        check_vma=False,
    )
```
